512 devices in a mesh: row: 16 (over x, z_hi, core), col: 32 (over y, z_lo).
Axes of the slice: x: 4, y: 4, z: 16 (z_hi: 2, z_lo: 8; z = z_hi * 8 + z_lo), core: 2. Of those that a mesh axis runs over, the one named last changes fastest.
Arguments:
- tokens: bfloat16 [16384, 16384], P('row', 'col'), may hold values from -6 to 6
- up_weight: bfloat16 [16384, 28672], P('row', 'col'), may hold values from -0.125 to 0.125
Outputs:
- projected: bfloat16 [16384, 28672], P('row', 'col')
The draws below stay inside these ranges and needn't reach their ends.
All inputs are finite; a program needn't handle non-finite values.
Results may differ from the reference program's by a relative error of at most 0.001.
Values may be sent and summed in bfloat16 or wider, within the bound.
A program may use at most 64 MiB of HBM per device.

```python
import jax
import jax.numpy as jnp
from jax import lax

D = 16384
FF = 28672
TB = 1024
TOKENS = 16384
BAND = 2048
N_ROW = 16


def levels(rng, extent, split, smallest, largest):
    loudness = 1.0
    for axis_at, parts in split:
        heights = jax.random.uniform(jax.random.fold_in(jax.random.fold_in(rng, 6), axis_at), (parts,), jnp.float32, smallest / len(split), largest / len(split))
        loudness = loudness * jnp.repeat(jnp.exp(heights), extent[axis_at] // parts).reshape((-1,) + (1,) * (len(extent) - 1 - axis_at))
    return loudness


def scatter_about(stream_key, extent, deviation, reach, split=(), held_as=jnp.bfloat16):
    array = deviation * jax.random.normal(stream_key, extent, jnp.float32)
    if split:
        array = array * levels(stream_key, extent, split, -0.22, 0.18)
    return jnp.clip(array, -reach, reach).astype(held_as)


def setup_inputs(seed: int = 0) -> dict:
    key_list = jax.random.split(jax.random.key(seed), 3)
    return {
        "tokens": scatter_about(key_list[0], (TOKENS, D), 1.0, 6.0, ((0, 16), (1, 32))),
        "up_weight": scatter_about(key_list[1], (D, FF), BAND ** -0.5, 0.125, ((0, 16), (1, 32))),
    }


def reference(tokens, up_weight):
    height = D // N_ROW

    def one_group(group):
        token_block = lax.dynamic_slice_in_dim(tokens, group * TB, TB, 0)
        following = (group + 1) % N_ROW
        first_part = jnp.dot(lax.dynamic_slice_in_dim(token_block, group * height, height, 1),
                             lax.dynamic_slice_in_dim(up_weight, group * height, height, 0),
                             preferred_element_type=jnp.float32)
        second_part = jnp.dot(lax.dynamic_slice_in_dim(token_block, following * height, height, 1),
                              lax.dynamic_slice_in_dim(up_weight, following * height, height, 0),
                              preferred_element_type=jnp.float32)
        return (first_part + second_part).astype(jnp.bfloat16)

    stacked = lax.map(one_group, jnp.arange(N_ROW, dtype=jnp.int32))
    return stacked.reshape(TOKENS, FF)
```

```python
import jax
import jax.numpy as jnp
from jax import lax
from jax.experimental import pallas as pl
from jax.experimental.pallas import tpu as pltpu
from jax.sharding import PartitionSpec as P

MESH = pl.DeviceIdType.MESH
ROWS, COLS = 16, 32
NY, NZ = 4, 8
PIECES = 4
SUBS = 2
WCHUNKS = 4


def kernel(tok, w, out, gath, land, w_own, w_next, acc, obuf,
           own_sem, w_send, w_recv, land_sem, gath_sem, s1_send, z_send, y_send, out_sem):
    row = lax.axis_index("row")
    col = lax.axis_index("col")
    core = lax.rem(row, 2)
    even = row - core
    y = col // NZ
    z = lax.rem(col, NZ)
    tokens = tok.shape[0]
    quarter = tokens // NY
    sub = quarter // SUBS
    depth = w.shape[0]
    wrows = depth // WCHUNKS
    piece_cols = tok.shape[1]
    per_piece = depth // piece_cols

    def at(y_, z_):
        return lax.rem(y_ + NY, NY) * NZ + z_

    def signal(r_, c_):
        pl.semaphore_signal(barrier, inc=1, device_id=(r_, c_), device_id_type=MESH)

    def piece_of(a, p):
        c_ = lax.rem(2 * (even + a) + p, COLS)
        return c_ // NZ, lax.rem(c_, NZ)

    def loop(n, f):
        lax.fori_loop(0, n, lambda i, carry: (f(i), carry)[1], 0)

    def rows_of(q, j):
        return pl.ds(pl.multiple_of(q * quarter + j * sub, sub), sub)

    def remote(src, dst, send, recv, r_, c_):
        return pltpu.make_async_remote_copy(
            src_ref=src, dst_ref=dst, send_sem=send, recv_sem=recv,
            device_id=(r_, c_), device_id_type=MESH)

    mine = lax.rem(col - 2 * row + 2 * COLS, COLS)
    is_source = mine < PIECES

    own_copy = pltpu.make_async_copy(w, w_own, own_sem)
    own_copy.start()

    def own_part(j):
        return pltpu.make_async_copy(
            tok.at[rows_of(y, j)], gath.at[mine, rows_of(y, j)], land_sem.at[1, mine, j])

    @pl.when(jnp.logical_and(core == 1, is_source))
    def _():
        loop(SUBS, lambda j: own_part(j).start())

    barrier = pltpu.get_barrier_semaphore()
    behind = lax.rem(row + ROWS - 1, ROWS)
    ahead = lax.rem(row + 1, ROWS)

    @pl.when(core == 0)
    def _():
        for dy in range(NY):
            signal(row + 1, at(y + dy, z))
        pl.semaphore_wait(barrier, NY + 1)

    @pl.when(core == 1)
    def _():
        signal(ahead, col)

        @pl.when(z > 0)
        def _():
            signal(row, at(y, z - 1))

        @pl.when(z < NZ - 1)
        def _():
            signal(row, at(y, z + 1))

        for dy in range(1, NY):
            signal(row, at(y + dy, z))
        for dy in range(NY):
            signal(row - 1, at(y + dy, z))
        middle = jnp.logical_and(z > 0, z < NZ - 1)
        pl.semaphore_wait(barrier, 2 * NY + jnp.where(middle, 1, 0))

    def s1_from0(q, j):
        return remote(tok.at[rows_of(q, j)], land.at[mine, pl.ds(j * sub, sub)],
                      s1_send.at[q, j], land_sem.at[0, mine, j], even + 1, at(q, z))

    def s1_from1(q, j):
        return remote(tok.at[rows_of(q, j)], gath.at[mine, rows_of(q, j)],
                      s1_send.at[q, j], land_sem.at[1, mine, j], row, at(q, z))

    def each_s1(act):
        @pl.when(jnp.logical_and(core == 0, is_source))
        def _():
            loop(SUBS, lambda j: loop(NY, lambda q: act(s1_from0(q, j))))

        @pl.when(jnp.logical_and(core == 1, is_source))
        def _():
            def one(q, j):
                @pl.when(q != y)
                def _():
                    act(s1_from1(q, j))
            loop(SUBS, lambda j: loop(NY, lambda q: one(q, j)))

    each_s1(lambda copy: copy.start())

    def w_copy(k):
        part = pl.ds(pl.multiple_of(k * wrows, wrows), wrows)
        return remote(w.at[part], w_next.at[part], w_send.at[k], w_recv.at[k], behind, col)

    loop(WCHUNKS, lambda k: w_copy(k).start())

    def relay_src(a, p, j):
        return land.at[p, pl.ds(j * sub, sub)] if a == 0 else gath.at[p, rows_of(y, j)]

    def z_copy(a, p, j, up):
        ref = relay_src(a, p, j)
        return remote(ref, ref, z_send.at[a, p, j, up], land_sem.at[a, p, j],
                      row, at(y, z + 1 if up else z - 1))

    def y_copy(a, p, j, dy):
        return remote(relay_src(a, p, j), gath.at[p, rows_of(y, j)],
                      y_send.at[a, p, j, dy], gath_sem.at[p, y, j], even + a, at(y + dy, z))

    def sends(a, p, j, zp, act):
        @pl.when(jnp.logical_and(z >= zp, z < NZ - 1))
        def _():
            act(z_copy(a, p, j, 1))

        @pl.when(jnp.logical_and(z <= zp, z > 0))
        def _():
            act(z_copy(a, p, j, 0))

        for dy in ((1, 3, 2) if a == 1 else (1, 3, 2, 0)):
            act(y_copy(a, p, j, dy))

    def arrived(a, p, j):
        ref = relay_src(a, p, j)
        return pltpu.make_async_copy(ref, ref, land_sem.at[a, p, j])

    @pl.when(core == 1)
    def _():
        def step(s):
            for a in (0, 1):
                def one(p, a=a):
                    zp = piece_of(a, p)[1]

                    @pl.when(jnp.abs(z - zp) == s)
                    def _():
                        def part(j):
                            arrived(a, p, j).wait()
                            sends(a, p, j, zp, lambda copy: copy.start())
                        loop(SUBS, part)
                loop(PIECES, one)
        loop(NZ, step)

    def have(p):
        def one(q):
            @pl.when(jnp.logical_or(core == 0, q != y))
            def _():
                def part(j):
                    ref = gath.at[p, rows_of(q, j)]
                    pltpu.make_async_copy(ref, ref, gath_sem.at[p, q, j]).wait()
                loop(SUBS, part)
        loop(NY, one)

    def q_rows(q):
        return pl.ds(pl.multiple_of(q * quarter, quarter), quarter)

    own_copy.wait()
    for p in range(per_piece):
        have(p)

    def first(q):
        total = jnp.dot(gath[0, q_rows(q)], w_own[:piece_cols], preferred_element_type=jnp.float32)
        for p in range(1, per_piece):
            total += jnp.dot(gath[p, q_rows(q)], w_own[p * piece_cols:(p + 1) * piece_cols],
                             preferred_element_type=jnp.float32)
        acc[q_rows(q)] = total
    loop(NY, first)

    def out_copy(q):
        return pltpu.make_async_copy(obuf.at[q_rows(q)], out.at[q_rows(q)], out_sem.at[q])

    for p in range(per_piece, PIECES):
        have(p)
    for k in range(WCHUNKS):
        w_copy(k).wait_recv()
        p = per_piece + k * wrows // piece_cols
        c0 = k * wrows % piece_cols

        def more(q):
            total = acc[q_rows(q)] + jnp.dot(
                gath[p, q_rows(q), c0:c0 + wrows], w_next[k * wrows:(k + 1) * wrows],
                preferred_element_type=jnp.float32)
            if k < WCHUNKS - 1:
                acc[q_rows(q)] = total
            else:
                obuf[q_rows(q)] = total.astype(obuf.dtype)
                out_copy(q).start()
        loop(NY, more)

    loop(NY, lambda q: out_copy(q).wait())
    loop(WCHUNKS, lambda k: w_copy(k).wait_send())
    each_s1(lambda copy: copy.wait_send())

    @pl.when(core == 1)
    def _():
        for a in (0, 1):
            def one(p, a=a):
                zp = piece_of(a, p)[1]
                loop(SUBS, lambda j: sends(a, p, j, zp, lambda copy: copy.wait_send()))
            loop(PIECES, one)


def body(tokens, up_weight):
    rows, cols = tokens.shape
    depth, width = up_weight.shape
    hbm = pl.BlockSpec(memory_space=pl.ANY)
    dma = pltpu.SemaphoreType.DMA
    bf16 = jnp.bfloat16
    return pl.pallas_call(
        kernel,
        out_shape=jax.ShapeDtypeStruct((rows, width), bf16),
        in_specs=[hbm, hbm],
        out_specs=hbm,
        scratch_shapes=[
            pltpu.VMEM((PIECES, rows, cols), bf16),
            pltpu.VMEM((PIECES, rows // NY, cols), bf16),
            pltpu.VMEM((depth, width), bf16),
            pltpu.VMEM((depth, width), bf16),
            pltpu.VMEM((rows, width), jnp.float32),
            pltpu.VMEM((rows, width), bf16),
            dma, dma((WCHUNKS,)), dma((WCHUNKS,)),
            dma((2, PIECES, SUBS)), dma((PIECES, NY, SUBS)), dma((NY, SUBS)),
            dma((2, PIECES, SUBS, 2)), dma((2, PIECES, SUBS, NY)), dma((NY,)),
        ],
        compiler_params=pltpu.CompilerParams(collective_id=0, has_side_effects=True),
        name="banded",
    )(tokens, up_weight)


def solution(mesh):
    placed = (P("row", "col"), P("row", "col"))
    return jax.shard_map(
        body, mesh=mesh, in_specs=placed, out_specs=P("row", "col"), check_vma=False
    )
```

```python
import jax
import jax.numpy as jnp
from jax import lax
from jax.experimental import pallas as pl
from jax.experimental.pallas import tpu as pltpu
from jax.sharding import PartitionSpec as P

MESH = pl.DeviceIdType.MESH
ROWS, COLS = 16, 32
NY, NZ = 4, 8
PIECES = 4
SUBS = 2
WCHUNKS = 8
HOPS = 8
NX, RING = 4, 16


def kernel(tok, w, out, gath, land, w_own, w_next, acc, obuf, held,
           own_sem, pair_send, pair_recv, f_send, h_send, h_recv, w_recv, land_sem, gath_sem, s1_send, z_send, y_send, out_sem):
    row = lax.axis_index("row")
    col = lax.axis_index("col")
    core = lax.rem(row, 2)
    even = row - core
    y = col // NZ
    z = lax.rem(col, NZ)
    tokens = tok.shape[0]
    quarter = tokens // NY
    sub = quarter // SUBS
    depth = w.shape[0]
    half = depth // 2
    wrows = half // WCHUNKS
    piece_cols = tok.shape[1]
    per_piece = depth // piece_cols

    def at(y_, z_):
        return lax.rem(y_ + NY, NY) * NZ + z_

    def signal(r_, c_):
        pl.semaphore_signal(barrier, inc=1, device_id=(r_, c_), device_id_type=MESH)

    def piece_of(a, p):
        c_ = lax.rem(2 * (even + a) + p, COLS)
        return c_ // NZ, lax.rem(c_, NZ)

    def loop(n, f):
        lax.fori_loop(0, n, lambda i, carry: (f(i), carry)[1], 0)

    def rows_of(q, j):
        return pl.ds(pl.multiple_of(q * quarter + j * sub, sub), sub)

    def remote(src, dst, send, recv, r_, c_):
        return pltpu.make_async_remote_copy(
            src_ref=src, dst_ref=dst, send_sem=send, recv_sem=recv,
            device_id=(r_, c_), device_id_type=MESH)

    mine = lax.rem(col - 2 * row + 2 * COLS, COLS)
    is_source = mine < PIECES

    own_copy = pltpu.make_async_copy(w, w_own, own_sem)
    own_copy.start()

    def own_part(j):
        return pltpu.make_async_copy(
            tok.at[rows_of(y, j)], gath.at[mine, rows_of(y, j)], land_sem.at[1, mine, j])

    @pl.when(jnp.logical_and(core == 1, is_source))
    def _():
        loop(SUBS, lambda j: own_part(j).start())

    x = row // (ROWS // NX)
    ring = NZ * lax.rem(row // 2, 2) + z
    near = (lax.rem(ring + 1, RING), lax.rem(ring + RING - 1, RING))

    def chip(x_, ring_, core_):
        return (x_ * 2 + ring_ // NZ) * 2 + core_, y * NZ + lax.rem(ring_, NZ)

    def x_from(ring_):
        return lax.rem(x + NX + jnp.where(ring_ < NZ, 1, 0), NX)

    x_to = lax.rem(x + NX - jnp.where(ring < NZ, 1, 0), NX)

    barrier = pltpu.get_barrier_semaphore()

    @pl.when(core == 0)
    def _():
        for n_ in near:
            signal(*chip(x_from(n_), n_, 0))
            signal(*chip(x, n_, 0))
        for dy in range(NY):
            signal(row + 1, at(y + dy, z))
        pl.semaphore_wait(barrier, NY + 6)

    @pl.when(core == 1)
    def _():
        for n_ in near:
            signal(*chip(x, n_, 0))

        @pl.when(z > 0)
        def _():
            signal(row, at(y, z - 1))

        @pl.when(z < NZ - 1)
        def _():
            signal(row, at(y, z + 1))

        for dy in range(1, NY):
            signal(row, at(y + dy, z))
        for dy in range(NY):
            signal(row - 1, at(y + dy, z))
        middle = jnp.logical_and(z > 0, z < NZ - 1)
        pl.semaphore_wait(barrier, 2 * NY + jnp.where(middle, 1, 0))

    def s1_from0(q, j):
        return remote(tok.at[rows_of(q, j)], land.at[mine, pl.ds(j * sub, sub)],
                      s1_send.at[q, j], land_sem.at[0, mine, j], even + 1, at(q, z))

    def s1_from1(q, j):
        return remote(tok.at[rows_of(q, j)], gath.at[mine, rows_of(q, j)],
                      s1_send.at[q, j], land_sem.at[1, mine, j], row, at(q, z))

    def each_s1(act):
        @pl.when(jnp.logical_and(core == 0, is_source))
        def _():
            loop(SUBS, lambda j: loop(NY, lambda q: act(s1_from0(q, j))))

        @pl.when(jnp.logical_and(core == 1, is_source))
        def _():
            def one(q, j):
                @pl.when(q != y)
                def _():
                    act(s1_from1(q, j))
            loop(SUBS, lambda j: loop(NY, lambda q: one(q, j)))

    each_s1(lambda copy: copy.start())

    def pair_copy():
        return remote(w, w_next, pair_send, pair_recv, even, col)

    def w_part(d, j):
        return pl.ds(pl.multiple_of(d * half + j * wrows, wrows), wrows)

    def first_hop(d, j):
        return remote(w.at[w_part(d, j)], held.at[d, 0, j], f_send.at[d, j], h_recv.at[d, 0, j],
                      *chip(x_to, near[d], 0))

    def next_hop(d, h, j):
        return remote(held.at[d, h - 1, j], held.at[d, h, j], h_send.at[d, h, j], h_recv.at[d, h, j],
                      *chip(x, near[d], 0))

    def last_hop(d, j):
        return remote(held.at[d, HOPS - 2, j], w_next.at[w_part(d, j)],
                      h_send.at[d, HOPS - 1, j], w_recv.at[d, j], *chip(x, near[d], 1))

    def held_in(d, h, j):
        ref = held.at[d, h, j]
        return pltpu.make_async_copy(ref, ref, h_recv.at[d, h, j])

    @pl.when(core == 1)
    def _():
        pair_copy().start()

    @pl.when(core == 0)
    def _():
        loop(WCHUNKS, lambda j: (first_hop(0, j).start(), first_hop(1, j).start()))

    def relay_src(a, p, j):
        return land.at[p, pl.ds(j * sub, sub)] if a == 0 else gath.at[p, rows_of(y, j)]

    def z_copy(a, p, j, up):
        ref = relay_src(a, p, j)
        return remote(ref, ref, z_send.at[a, p, j, up], land_sem.at[a, p, j],
                      row, at(y, z + 1 if up else z - 1))

    def y_copy(a, p, j, dy):
        return remote(relay_src(a, p, j), gath.at[p, rows_of(y, j)],
                      y_send.at[a, p, j, dy], gath_sem.at[p, y, j], even + a, at(y + dy, z))

    def sends(a, p, j, zp, act):
        @pl.when(jnp.logical_and(z >= zp, z < NZ - 1))
        def _():
            act(z_copy(a, p, j, 1))

        @pl.when(jnp.logical_and(z <= zp, z > 0))
        def _():
            act(z_copy(a, p, j, 0))

        for dy in ((1, 3, 2) if a == 1 else (1, 3, 2, 0)):
            act(y_copy(a, p, j, dy))

    def arrived(a, p, j):
        ref = relay_src(a, p, j)
        return pltpu.make_async_copy(ref, ref, land_sem.at[a, p, j])

    @pl.when(core == 1)
    def _():
        def step(s):
            for a in (0, 1):
                def one(p, a=a):
                    zp = piece_of(a, p)[1]

                    @pl.when(jnp.abs(z - zp) == s)
                    def _():
                        def part(j):
                            arrived(a, p, j).wait()
                            sends(a, p, j, zp, lambda copy: copy.start())
                        loop(SUBS, part)
                loop(PIECES, one)
        loop(NZ, step)

    def have(p):
        def one(q):
            @pl.when(jnp.logical_or(core == 0, q != y))
            def _():
                def part(j):
                    ref = gath.at[p, rows_of(q, j)]
                    pltpu.make_async_copy(ref, ref, gath_sem.at[p, q, j]).wait()
                loop(SUBS, part)
        loop(NY, one)

    def q_rows(q):
        return pl.ds(pl.multiple_of(q * quarter, quarter), quarter)

    def out_copy(q):
        return pltpu.make_async_copy(obuf.at[q_rows(q)], out.at[q_rows(q)], out_sem.at[q])

    def product(p, q, weights, r0, rows):
        c0 = r0 % piece_cols
        return jnp.dot(gath[p, q_rows(q), c0:c0 + rows], weights[r0:r0 + rows],
                       preferred_element_type=jnp.float32)

    def own_product(q):
        total = product(0, q, w_own, 0, piece_cols)
        for p in range(1, per_piece):
            total += product(p, q, w_own, p * piece_cols, piece_cols)
        return total

    @pl.when(core == 0)
    def _():
        def pass_on(h):
            def one(j):
                for d in (0, 1):
                    held_in(d, h - 1, j).wait()
                    next_hop(d, h, j).start()
            loop(WCHUNKS, one)
        lax.fori_loop(1, HOPS - 1, lambda h, c: (pass_on(h), c)[1], 0)

        def finish(j):
            for d in (0, 1):
                held_in(d, HOPS - 2, j).wait()
                last_hop(d, j).start()
        loop(WCHUNKS, finish)

        own_copy.wait()
        pair_copy().wait_recv()
        for p in range(PIECES):
            have(p)

        def whole(q):
            total = own_product(q)
            for p in range(per_piece, PIECES):
                total += product(p, q, w_next, (p - per_piece) * piece_cols, piece_cols)
            obuf[q_rows(q)] = total.astype(obuf.dtype)
            out_copy(q).start()
        loop(NY, whole)

    @pl.when(core == 1)
    def _():
        own_copy.wait()
        for p in range(PIECES):
            have(p)

        def begin(q):
            acc[q_rows(q)] = own_product(q)
        loop(NY, begin)

        groups = 2
        for g in range(groups):
            span = half // groups

            def got(j):
                for d in (0, 1):
                    ref = w_next.at[w_part(d, j)]
                    pltpu.make_async_copy(ref, ref, w_recv.at[d, j]).wait()
            lax.fori_loop(g * WCHUNKS // groups, (g + 1) * WCHUNKS // groups, lambda j, c: (got(j), c)[1], 0)

            def more(q):
                total = acc[q_rows(q)]
                for d in (0, 1):
                    r0 = d * half + g * span
                    total += product(per_piece + r0 // piece_cols, q, w_next, r0, span)
                if g < groups - 1:
                    acc[q_rows(q)] = total
                else:
                    obuf[q_rows(q)] = total.astype(obuf.dtype)
                    out_copy(q).start()
            loop(NY, more)

    loop(NY, lambda q: out_copy(q).wait())

    @pl.when(core == 0)
    def _():
        def sent(j):
            for d in (0, 1):
                first_hop(d, j).wait_send()
                lax.fori_loop(1, HOPS - 1, lambda h, c: (next_hop(d, h, j).wait_send(), c)[1], 0)
                last_hop(d, j).wait_send()
        loop(WCHUNKS, sent)

    @pl.when(core == 1)
    def _():
        pair_copy().wait_send()

    each_s1(lambda copy: copy.wait_send())

    @pl.when(core == 1)
    def _():
        for a in (0, 1):
            def one(p, a=a):
                zp = piece_of(a, p)[1]
                loop(SUBS, lambda j: sends(a, p, j, zp, lambda copy: copy.wait_send()))
            loop(PIECES, one)


def body(tokens, up_weight):
    rows, cols = tokens.shape
    depth, width = up_weight.shape
    hbm = pl.BlockSpec(memory_space=pl.ANY)
    dma = pltpu.SemaphoreType.DMA
    bf16 = jnp.bfloat16
    return pl.pallas_call(
        kernel,
        out_shape=jax.ShapeDtypeStruct((rows, width), bf16),
        in_specs=[hbm, hbm],
        out_specs=hbm,
        scratch_shapes=[
            pltpu.VMEM((PIECES, rows, cols), bf16),
            pltpu.VMEM((PIECES, rows // NY, cols), bf16),
            pltpu.VMEM((depth, width), bf16),
            pltpu.VMEM((depth, width), bf16),
            pltpu.VMEM((rows, width), jnp.float32),
            pltpu.VMEM((rows, width), bf16),
            pltpu.VMEM((2, HOPS - 1, WCHUNKS, depth // (2 * WCHUNKS), width), bf16),
            dma, dma, dma, dma((2, WCHUNKS)), dma((2, HOPS, WCHUNKS)), dma((2, HOPS - 1, WCHUNKS)),
            dma((2, WCHUNKS)),
            dma((2, PIECES, SUBS)), dma((PIECES, NY, SUBS)), dma((NY, SUBS)),
            dma((2, PIECES, SUBS, 2)), dma((2, PIECES, SUBS, NY)), dma((NY,)),
        ],
        compiler_params=pltpu.CompilerParams(collective_id=0, has_side_effects=True),
        name="banded",
    )(tokens, up_weight)


def solution(mesh):
    placed = (P("row", "col"), P("row", "col"))
    return jax.shard_map(
        body, mesh=mesh, in_specs=placed, out_specs=P("row", "col"), check_vma=False
    )
```

```python
import jax
import jax.numpy as jnp
from jax import lax
from jax.experimental import pallas as pl
from jax.experimental.pallas import tpu as pltpu
from jax.sharding import PartitionSpec as P

MESH = pl.DeviceIdType.MESH
ROWS, COLS = 16, 32
NY, NZ = 4, 8
PIECES = 4
SUBS = 2
WCHUNKS = 8
HOPS = 8
NX, RING = 4, 16


def kernel(tok, w, out, gath, land, w_own, w_next, acc, held,
           own_sem, pair_send, pair_recv, f_send, h_send, h_recv, w_recv, land_sem, gath_sem, s1_send, z_send, y_send):
    row = lax.axis_index("row")
    col = lax.axis_index("col")
    core = lax.rem(row, 2)
    even = row - core
    y = col // NZ
    z = lax.rem(col, NZ)
    tokens = tok.shape[0]
    quarter = tokens // NY
    sub = quarter // SUBS
    depth = w.shape[0]
    half = depth // 2
    wrows = half // WCHUNKS
    piece_cols = tok.shape[1]
    per_piece = depth // piece_cols

    def at(y_, z_):
        return lax.rem(y_ + NY, NY) * NZ + z_

    def signal(r_, c_):
        pl.semaphore_signal(barrier, inc=1, device_id=(r_, c_), device_id_type=MESH)

    def piece_of(a, p):
        c_ = lax.rem(2 * (even + a) + p, COLS)
        return c_ // NZ, lax.rem(c_, NZ)

    def loop(n, f):
        lax.fori_loop(0, n, lambda i, carry: (f(i), carry)[1], 0)

    def rows_of(q, j):
        return pl.ds(pl.multiple_of(q * quarter + j * sub, sub), sub)

    def remote(src, dst, send, recv, r_, c_):
        return pltpu.make_async_remote_copy(
            src_ref=src, dst_ref=dst, send_sem=send, recv_sem=recv,
            device_id=(r_, c_), device_id_type=MESH)

    mine = lax.rem(col - 2 * row + 2 * COLS, COLS)
    is_source = mine < PIECES

    own_copy = pltpu.make_async_copy(w, w_own, own_sem)
    own_copy.start()

    def own_part(j):
        return pltpu.make_async_copy(
            tok.at[rows_of(y, j)], gath.at[mine, rows_of(y, j)], land_sem.at[1, mine, j])

    @pl.when(jnp.logical_and(core == 1, is_source))
    def _():
        loop(SUBS, lambda j: own_part(j).start())

    x = row // (ROWS // NX)
    ring = NZ * lax.rem(row // 2, 2) + z
    near = (lax.rem(ring + 1, RING), lax.rem(ring + RING - 1, RING))

    def chip(x_, ring_, core_):
        return (x_ * 2 + ring_ // NZ) * 2 + core_, y * NZ + lax.rem(ring_, NZ)

    def x_from(ring_):
        return lax.rem(x + NX + jnp.where(ring_ < NZ, 1, 0), NX)

    x_to = lax.rem(x + NX - jnp.where(ring < NZ, 1, 0), NX)

    barrier = pltpu.get_barrier_semaphore()

    @pl.when(core == 0)
    def _():
        for n_ in near:
            signal(*chip(x_from(n_), n_, 0))
            signal(*chip(x, n_, 0))
        for dy in range(NY):
            signal(row + 1, at(y + dy, z))
        pl.semaphore_wait(barrier, NY + 6)

    @pl.when(core == 1)
    def _():
        for n_ in near:
            signal(*chip(x, n_, 0))

        @pl.when(z > 0)
        def _():
            signal(row, at(y, z - 1))

        @pl.when(z < NZ - 1)
        def _():
            signal(row, at(y, z + 1))

        for dy in range(1, NY):
            signal(row, at(y + dy, z))
        for dy in range(NY):
            signal(row - 1, at(y + dy, z))
        middle = jnp.logical_and(z > 0, z < NZ - 1)
        pl.semaphore_wait(barrier, 2 * NY + jnp.where(middle, 1, 0))

    def s1_from0(q, j):
        return remote(tok.at[rows_of(q, j)], land.at[mine, pl.ds(j * sub, sub)],
                      s1_send.at[q, j], land_sem.at[0, mine, j], even + 1, at(q, z))

    def s1_from1(q, j):
        return remote(tok.at[rows_of(q, j)], gath.at[mine, rows_of(q, j)],
                      s1_send.at[q, j], land_sem.at[1, mine, j], row, at(q, z))

    def each_s1(act):
        @pl.when(jnp.logical_and(core == 0, is_source))
        def _():
            loop(SUBS, lambda j: loop(NY, lambda q: act(s1_from0(q, j))))

        @pl.when(jnp.logical_and(core == 1, is_source))
        def _():
            def one(q, j):
                @pl.when(q != y)
                def _():
                    act(s1_from1(q, j))
            loop(SUBS, lambda j: loop(NY, lambda q: one(q, j)))

    each_s1(lambda copy: copy.start())

    def pair_copy():
        return remote(w, w_next, pair_send, pair_recv, even, col)

    def w_part(d, j):
        return pl.ds(pl.multiple_of(d * half + j * wrows, wrows), wrows)

    def first_hop(d, j):
        return remote(w.at[w_part(d, j)], held.at[d, 0, j], f_send.at[d, j], h_recv.at[d, 0, j],
                      *chip(x_to, near[d], 0))

    def next_hop(d, h, j):
        return remote(held.at[d, h - 1, j], held.at[d, h, j], h_send.at[d, h, j], h_recv.at[d, h, j],
                      *chip(x, near[d], 0))

    def last_hop(d, j):
        return remote(held.at[d, HOPS - 2, j], w_next.at[w_part(d, j)],
                      h_send.at[d, HOPS - 1, j], w_recv.at[d, j], *chip(x, near[d], 1))

    def held_in(d, h, j):
        ref = held.at[d, h, j]
        return pltpu.make_async_copy(ref, ref, h_recv.at[d, h, j])

    @pl.when(core == 1)
    def _():
        pair_copy().start()

    @pl.when(core == 0)
    def _():
        loop(WCHUNKS, lambda j: (first_hop(0, j).start(), first_hop(1, j).start()))

    def relay_src(a, p, j):
        return land.at[p, pl.ds(j * sub, sub)] if a == 0 else gath.at[p, rows_of(y, j)]

    def z_copy(a, p, j, up):
        ref = relay_src(a, p, j)
        return remote(ref, ref, z_send.at[a, p, j, up], land_sem.at[a, p, j],
                      row, at(y, z + 1 if up else z - 1))

    def y_copy(a, p, j, dy):
        return remote(relay_src(a, p, j), gath.at[p, rows_of(y, j)],
                      y_send.at[a, p, j, dy], gath_sem.at[p, y, j], even + a, at(y + dy, z))

    def sends(a, p, j, zp, act):
        @pl.when(jnp.logical_and(z >= zp, z < NZ - 1))
        def _():
            act(z_copy(a, p, j, 1))

        @pl.when(jnp.logical_and(z <= zp, z > 0))
        def _():
            act(z_copy(a, p, j, 0))

        for dy in ((1, 3, 2) if a == 1 else (1, 3, 2, 0)):
            act(y_copy(a, p, j, dy))

    def arrived(a, p, j):
        ref = relay_src(a, p, j)
        return pltpu.make_async_copy(ref, ref, land_sem.at[a, p, j])

    @pl.when(core == 1)
    def _():
        def step(s):
            for a in (0, 1):
                def one(p, a=a):
                    zp = piece_of(a, p)[1]

                    @pl.when(jnp.abs(z - zp) == s)
                    def _():
                        def part(j):
                            arrived(a, p, j).wait()
                            sends(a, p, j, zp, lambda copy: copy.start())
                        loop(SUBS, part)
                loop(PIECES, one)
        loop(NZ, step)

    def have(p):
        def one(q):
            @pl.when(jnp.logical_or(core == 0, q != y))
            def _():
                def part(j):
                    ref = gath.at[p, rows_of(q, j)]
                    pltpu.make_async_copy(ref, ref, gath_sem.at[p, q, j]).wait()
                loop(SUBS, part)
        loop(NY, one)

    def q_rows(q):
        return pl.ds(pl.multiple_of(q * quarter, quarter), quarter)

    def product(p, q, weights, r0, rows):
        c0 = r0 % piece_cols
        return jnp.dot(gath[p, q_rows(q), c0:c0 + rows], weights[r0:r0 + rows],
                       preferred_element_type=jnp.float32)

    def own_product(q):
        total = product(0, q, w_own, 0, piece_cols)
        for p in range(1, per_piece):
            total += product(p, q, w_own, p * piece_cols, piece_cols)
        return total

    @pl.when(core == 0)
    def _():
        def pass_on(h):
            def one(j):
                for d in (0, 1):
                    held_in(d, h - 1, j).wait()
                    next_hop(d, h, j).start()
            loop(WCHUNKS, one)
        lax.fori_loop(1, HOPS - 1, lambda h, c: (pass_on(h), c)[1], 0)

        def finish(j):
            for d in (0, 1):
                held_in(d, HOPS - 2, j).wait()
                last_hop(d, j).start()
        loop(WCHUNKS, finish)

        own_copy.wait()
        pair_copy().wait_recv()
        for p in range(PIECES):
            have(p)

        def whole(q):
            total = own_product(q)
            for p in range(per_piece, PIECES):
                total += product(p, q, w_next, (p - per_piece) * piece_cols, piece_cols)
            out[q_rows(q)] = total.astype(out.dtype)
        loop(NY, whole)

    @pl.when(core == 1)
    def _():
        own_copy.wait()
        for p in range(PIECES):
            have(p)

        def begin(q):
            acc[q_rows(q)] = own_product(q)
        loop(NY, begin)

        groups = 2
        for g in range(groups):
            span = half // groups

            def got(j):
                for d in (0, 1):
                    ref = w_next.at[w_part(d, j)]
                    pltpu.make_async_copy(ref, ref, w_recv.at[d, j]).wait()
            lax.fori_loop(g * WCHUNKS // groups, (g + 1) * WCHUNKS // groups, lambda j, c: (got(j), c)[1], 0)

            def more(q):
                total = acc[q_rows(q)]
                for d in (0, 1):
                    r0 = d * half + g * span
                    total += product(per_piece + r0 // piece_cols, q, w_next, r0, span)
                if g < groups - 1:
                    acc[q_rows(q)] = total
                else:
                    out[q_rows(q)] = total.astype(out.dtype)
            loop(NY, more)


    @pl.when(core == 0)
    def _():
        def sent(j):
            for d in (0, 1):
                first_hop(d, j).wait_send()
                lax.fori_loop(1, HOPS - 1, lambda h, c: (next_hop(d, h, j).wait_send(), c)[1], 0)
                last_hop(d, j).wait_send()
        loop(WCHUNKS, sent)

    @pl.when(core == 1)
    def _():
        pair_copy().wait_send()

    each_s1(lambda copy: copy.wait_send())

    @pl.when(core == 1)
    def _():
        for a in (0, 1):
            def one(p, a=a):
                zp = piece_of(a, p)[1]
                loop(SUBS, lambda j: sends(a, p, j, zp, lambda copy: copy.wait_send()))
            loop(PIECES, one)


def body(tokens, up_weight):
    rows, cols = tokens.shape
    depth, width = up_weight.shape
    hbm = pl.BlockSpec(memory_space=pl.ANY)
    dma = pltpu.SemaphoreType.DMA
    bf16 = jnp.bfloat16
    tokens = pltpu.with_memory_space_constraint(tokens, pltpu.HBM)
    up_weight = pltpu.with_memory_space_constraint(up_weight, pltpu.HBM)
    return pl.pallas_call(
        kernel,
        out_shape=jax.ShapeDtypeStruct((rows, width), bf16),
        in_specs=[pl.BlockSpec(memory_space=pltpu.HBM)] * 2,
        out_specs=pl.BlockSpec(memory_space=pltpu.VMEM),
        scratch_shapes=[
            pltpu.VMEM((PIECES, rows, cols), bf16),
            pltpu.VMEM((PIECES, rows // NY, cols), bf16),
            pltpu.VMEM((depth, width), bf16),
            pltpu.VMEM((depth, width), bf16),
            pltpu.VMEM((rows, width), jnp.float32),
            pltpu.VMEM((2, HOPS - 1, WCHUNKS, depth // (2 * WCHUNKS), width), bf16),
            dma, dma, dma, dma((2, WCHUNKS)), dma((2, HOPS, WCHUNKS)), dma((2, HOPS - 1, WCHUNKS)),
            dma((2, WCHUNKS)),
            dma((2, PIECES, SUBS)), dma((PIECES, NY, SUBS)), dma((NY, SUBS)),
            dma((2, PIECES, SUBS, 2)), dma((2, PIECES, SUBS, NY)),
        ],
        compiler_params=pltpu.CompilerParams(collective_id=0, has_side_effects=True, vmem_limit_bytes=32<<20),
        name="banded",
    )(tokens, up_weight)


def solution(mesh):
    placed = (P("row", "col"), P("row", "col"))
    return jax.shard_map(
        body, mesh=mesh, in_specs=placed, out_specs=P("row", "col"), check_vma=False
    )
```
